32 devices in a mesh: img: 2 (over core), row: 2 (over x), col: 8 (over z, y).
Axes of the slice: x: 2, y: 2, z: 4, core: 2. Of those that a mesh axis runs over, the one named last changes fastest.
Arguments:
- images: bfloat16 [8, 32, 128], P('img', 'row', 'col'), may hold values from -4 to 4
- filters: bfloat16 [64, 9, 9], replicated, may hold values from -0.625 to 0.625
- hidden_bias: float32 [64], replicated, may hold values from -3 to -1
- visible_unit_bias: float32 [], replicated, may hold values from -0.5 to 0.5
- unit_noise: bfloat16 [8, 32, 8192], P('img', 'row', 'col'), may hold values from 0.019897461 to 0.9765625
Outputs:
- recon: bfloat16 [8, 32, 128], P('img', 'row', 'col')
- grad_filters: float32 [64, 9, 9], replicated
- grad_hidden: float32 [64], replicated
- grad_visible: float32 [], replicated
The draws below stay inside these ranges and needn't reach their ends.
All inputs are finite; a program needn't handle non-finite values.
Results may differ from the reference program's by a relative error of at most 0.0075.
Values may be sent and summed in bfloat16 or wider, within the bound.
A program may use at most 64 MiB of HBM per device.

```python
import jax
import jax.numpy as jnp
from jax import lax

K = 64
FILT = 9
B = 8
H = 32
W = 128


def level_of(own_key, extent, pieces, least, high):
    def one(axis_at, parts):
        steps = jax.random.uniform(jax.random.fold_in(jax.random.fold_in(own_key, 6), axis_at), (parts,), jnp.float32, least / len(pieces), high / len(pieces))
        return jnp.repeat(jnp.exp(steps), extent[axis_at] // parts).reshape((-1,) + (1,) * (len(extent) - axis_at - 1))

    loudness = one(*pieces[0])
    for cut in pieces[1:]:
        loudness = loudness * one(*cut)
    return loudness


def gaussian(stream_key, shape, deviation, most, cuts=(), dtype=jnp.bfloat16):
    array = deviation * jax.random.normal(stream_key, shape, jnp.float32)
    if cuts:
        array = array * level_of(stream_key, shape, cuts, -0.22, 0.18)
    return jnp.clip(array, -most, most).astype(dtype)


def setup_inputs(seed: int = 0) -> dict:
    arg_keys = jax.random.split(jax.random.key(seed), 6)
    return {
        "images": gaussian(arg_keys[0], (B, H, W), 1.0, 4.0, ((0, 2), (1, 2), (2, 8))),
        "filters": gaussian(arg_keys[1], (K, FILT, FILT), (FILT * FILT) ** -0.5, 0.625),
        "hidden_bias": jnp.clip(jax.random.uniform(arg_keys[2], (K,), jnp.float32, -3.0, -1.0), -3.0, -1.0),
        "visible_unit_bias": jnp.clip(jax.random.uniform(arg_keys[3], (), jnp.float32, -0.5, 0.5), -0.5, 0.5),
        "unit_noise": jnp.clip(0.019897461 + 0.95666504 * jax.random.uniform(arg_keys[4], (B, H, W * K), jnp.float32) ** level_of(arg_keys[4], (B, H, W * K), ((0, 2), (1, 2), (2, 8)), -0.2, 0.2), 0.019897461, 0.9765625).astype(jnp.bfloat16),
    }


relaxation_coldness = 0.5


def group_peak_odds(binary_hidden_outcome):
    axis_ordering = binary_hidden_outcome.shape
    lifted_power = jnp.exp(binary_hidden_outcome).reshape(axis_ordering[0], axis_ordering[1], axis_ordering[2] // 2, 2, axis_ordering[3] // 2, 2)
    denominator = 1.0 + jnp.sum(lifted_power, axis=(3, 5), keepdims=True)
    return (lifted_power / denominator).reshape(axis_ordering)


def smoothed_draw(binary_hidden_outcome, flat_random_numbers):
    random_jitter_draw = -jnp.log(-jnp.log(flat_random_numbers.astype(jnp.float32)))
    return group_peak_odds((binary_hidden_outcome + random_jitter_draw) / relaxation_coldness).astype(jnp.bfloat16)


def cross_correlate(source, kernels, margin):
    return lax.conv_general_dilated(source, kernels, (1, 1), ((margin, margin), (margin, margin)), dimension_numbers=("NCHW", "OIHW", "NCHW"), preferred_element_type=jnp.float32)


def filter_terms(source, hidden_map, margin):
    return lax.conv_general_dilated(source, hidden_map, (1, 1), ((margin, margin), (margin, margin)), dimension_numbers=("NCHW", "IOHW", "NCHW"), preferred_element_type=jnp.float32)[0]


def reference(images, filters, hidden_bias, visible_unit_bias, unit_noise):
    margin = FILT // 2
    kernels = filters[:, None]
    flipped = filters[None, :, ::-1, ::-1]
    bias_map = hidden_bias[None, :, None, None]

    def one_image(inputs):
        visible, noise_flat = inputs
        flat_random_numbers = noise_flat.reshape(H, W, K).transpose(2, 0, 1)
        source = visible[None, None]
        positive = cross_correlate(source, kernels, margin) + bias_map
        pos_prob = group_peak_odds(positive)
        sample = smoothed_draw(positive, flat_random_numbers[None])
        recon = (cross_correlate(sample, flipped, margin)[0, 0] + visible_unit_bias).astype(jnp.bfloat16)
        model_phase_statistics = cross_correlate(recon[None, None], kernels, margin) + bias_map
        neg_prob = group_peak_odds(model_phase_statistics)
        filter_sum = filter_terms(source, pos_prob.astype(jnp.bfloat16), margin) - filter_terms(recon[None, None], neg_prob.astype(jnp.bfloat16), margin)
        hidden_sum = jnp.sum(pos_prob - neg_prob, axis=(0, 2, 3))
        visible_sum = jnp.sum(visible.astype(jnp.float32) - recon.astype(jnp.float32))
        return recon, filter_sum, hidden_sum, visible_sum

    recon, filter_sums, hidden_sums, visible_sums = lax.map(one_image, (images, unit_noise))
    scale = 1.0 / (B * H * W)
    return recon, jnp.sum(filter_sums, axis=0) * scale, jnp.sum(hidden_sums, axis=0) * scale, jnp.sum(visible_sums) * scale
```

```python
import functools

import jax
import jax.numpy as jnp
from jax import lax
from jax.experimental import pallas as pl
from jax.experimental.pallas import tpu as pltpu
from jax.sharding import PartitionSpec as P

LANES = 128
MESH = pl.DeviceIdType.MESH
DIRS = [(dr, dc) for dr in (-1, 0, 1) for dc in (-1, 0, 1) if (dr, dc) != (0, 0)]
f32 = jnp.float32
bf16 = jnp.bfloat16


def slot_of(dr, dc):
    return (dr + 1) * 3 + dc + 1


def pooled(e):
    rows = e.shape[0]
    s = e + pltpu.roll(e, LANES // 2, axis=1)
    s3 = s.reshape(rows // 8, 8, LANES)
    even = lax.broadcasted_iota(jnp.int32, s3.shape, 1) % 2 == 0
    t3 = jnp.where(even, pltpu.roll(s3, 7, axis=1), pltpu.roll(s3, 1, axis=1))
    return 1.0 + s + t3.reshape(rows, LANES)


def kernel(
    geo, img_ref, fil_ref, hb_ref, vb_ref, noise_ref, recon_ref, c_out_ref,
    pf, pack, recv_img, ext, a_ref, fp, tz, w_ref, h_ref, s_ref, u_ref, e_ref, recv_e,
    g_ref, acc_ref, c_ref, recv1, recv2, is_sem, ir_sem, es_sem, er_sem, s1_sem, r1_sem, s2_sem, r2_sem,
):
    ni, th, tw, k, filt, n_img, n_row, n_col = geo
    m = filt // 2
    eh, ew = th + 2 * m, tw + 2 * m
    stride = LANES // ni
    rows = ni * th
    blocks = tw * k // LANES
    kp = a_ref.shape[1]
    img_at, row_at, col_at = lax.axis_index("img"), lax.axis_index("row"), lax.axis_index("col")
    n1, n2 = n_img * n_row, n_col
    me1, me2 = img_at * n_row + row_at, col_at

    def exists(dr, dc):
        ok = True
        if dr:
            ok = (row_at > 0) if dr < 0 else (row_at < n_row - 1)
        if dc:
            ok2 = (col_at > 0) if dc < 0 else (col_at < n_col - 1)
            ok = jnp.logical_and(ok, ok2) if dr else ok2
        return ok

    def neighbour(dr, dc):
        return {"row": row_at + dr, "col": col_at + dc}

    def group1(d):
        other = lax.rem(me1 + d, n1)
        return other, {"img": other // n_row, "row": lax.rem(other, n_row)}

    def group2(d):
        other = lax.rem(me2 + d, n2)
        return other, {"col": other}

    recv_img[...] = jnp.zeros_like(recv_img)
    recv_e[...] = jnp.zeros_like(recv_e)
    barrier = pltpu.get_barrier_semaphore()
    count = jnp.int32(n1 - 1 + n2 - 1)
    for d in DIRS:
        @pl.when(exists(*d))
        def _(d=d):
            pl.semaphore_signal(barrier, inc=1, device_id=neighbour(*d), device_id_type=MESH)
        count = count + exists(*d).astype(jnp.int32)
    for d in range(1, n1):
        pl.semaphore_signal(barrier, inc=1, device_id=group1(d)[1], device_id_type=MESH)
    for d in range(1, n2):
        pl.semaphore_signal(barrier, inc=1, device_id=group2(d)[1], device_id_type=MESH)

    pf[...] = jnp.zeros_like(pf)
    for n in range(ni):
        pf[:, n * stride + m : n * stride + m + tw] = img_ref[n].astype(f32)
    pack[...] = pf[...].astype(bf16)

    top = fp.shape[0] - kp
    q = fil_ref.shape[0]
    fp[...] = jnp.zeros_like(fp)
    fv = fil_ref[...].astype(f32)
    per = LANES // k
    for jp in range(per):
        fp[top + jp : top + jp + q, jp * k : (jp + 1) * k] = fv
    pl.semaphore_wait(barrier, count)

    def exchange(make, start):
        for d in DIRS:
            @pl.when(exists(*d))
            def _(d=d):
                cp = make(*d)
                if start:
                    cp.start()
                else:
                    cp.wait()

    def img_copy(dr, dc, start):
        at = slot_of(-dr, -dc) if start else slot_of(dr, dc)
        return pltpu.make_async_remote_copy(
            src_ref=pack, dst_ref=recv_img.at[at], send_sem=is_sem.at[at], recv_sem=ir_sem.at[at],
            device_id=neighbour(dr, dc), device_id_type=MESH,
        )

    for d in DIRS:
        @pl.when(exists(*d))
        def _(d=d):
            img_copy(*d, True).start()

    for b in range(blocks):
        tz[:, b * LANES : (b + 1) * LANES] = fp[top - per * b : top - per * b + kp, :].astype(bf16)
        w_ref[:, b * LANES : (b + 1) * LANES] = 1.0 / jnp.log(noise_ref[:, b * LANES : (b + 1) * LANES].astype(f32))
    a_ref[...] = jnp.zeros_like(a_ref)

    lane = lax.broadcasted_iota(jnp.int32, (th, LANES), 1) % stride

    def place(a_row):
        for n in range(ni):
            for r in range(filt):
                a_ref[a_row + n * th : a_row + (n + 1) * th, r * ew : (r + 1) * ew] = ext[
                    r : r + th, n * stride : n * stride + ew
                ]

    for d in DIRS:
        @pl.when(exists(*d))
        def _(d=d):
            img_copy(*d, True).wait_send()
            img_copy(*d, False).wait_recv()

    for dr in (-1, 0, 1):
        centre = pf[...] if dr == 0 else recv_img[slot_of(dr, 0)].astype(f32)
        left = pltpu.roll(recv_img[slot_of(dr, -1)].astype(f32), LANES - tw, axis=1)
        right = pltpu.roll(recv_img[slot_of(dr, 1)].astype(f32), tw, axis=1)
        band = jnp.where(lane < m, left, jnp.where(lane < m + tw, centre, jnp.where(lane < ew, right, 0.0)))
        if dr == 0:
            ext[m : m + th, :] = band
        elif dr < 0:
            ext[0:m, :] = band[th - m :, :]
        else:
            ext[m + th :, :] = band[:m, :]
    place(0)

    bias = jnp.concatenate([hb_ref[...]] * per, axis=1)
    a_pos = a_ref[0:rows, :].astype(bf16)
    hidden = jnp.zeros((8, LANES), f32)

    def fold(x):
        return jnp.sum(x.reshape(rows // 8, 8, LANES), axis=0)

    step = 2 * LANES if blocks % 2 == 0 else LANES
    for b0 in range(0, blocks * LANES, step):
        xw = jnp.dot(a_pos, tz[:, b0 : b0 + step], preferred_element_type=f32)
        for o in range(0, step, LANES):
            at = b0 + o
            e = jnp.exp(xw[:, o : o + LANES] + bias)
            prob = e / pooled(e)
            hidden = hidden + fold(prob)
            h_ref[0:rows, at : at + LANES] = prob.astype(bf16)
            t = e * w_ref[:, at : at + LANES]
            t = t * t
            s_ref[:, at : at + LANES] = (t / pooled(t)).astype(bf16)

    u_ref[...] = lax.dot_general(s_ref[...], tz[...], (((1,), (1,)), ((), ())), preferred_element_type=f32)
    e_ref[...] = jnp.zeros_like(e_ref)
    gap = jnp.zeros((th, stride - ew), f32)
    for r in range(filt):
        pieces = []
        for n in range(ni):
            pieces += [u_ref[n * th : (n + 1) * th, r * ew : (r + 1) * ew], gap]
        e_ref[r : r + th, :] += jnp.concatenate(pieces, axis=1)

    def e_copy(dr, dc, start):
        at = slot_of(-dr, -dc) if start else slot_of(dr, dc)
        way = dr if start else -dr
        if way == 0:
            src, dst = e_ref, recv_e.at[at]
        elif way > 0:
            src, dst = e_ref.at[th:eh], recv_e.at[at, 0 : 2 * m]
        else:
            src, dst = e_ref.at[0 : 2 * m], recv_e.at[at, th:eh]
        return pltpu.make_async_remote_copy(
            src_ref=src, dst_ref=dst, send_sem=es_sem.at[at], recv_sem=er_sem.at[at],
            device_id=neighbour(dr, dc), device_id_type=MESH,
        )

    for d in DIRS:
        @pl.when(exists(*d))
        def _(d=d):
            e_copy(*d, True).start()
    for d in DIRS:
        @pl.when(exists(*d))
        def _(d=d):
            e_copy(*d, True).wait_send()
            e_copy(*d, False).wait_recv()

    elane = lax.broadcasted_iota(jnp.int32, (eh, LANES), 1) % stride
    erow = lax.broadcasted_iota(jnp.int32, (eh, LANES), 0)
    total = e_ref[...] + recv_e[slot_of(-1, 0)] + recv_e[slot_of(1, 0)]
    left = recv_e[slot_of(-1, -1)] + recv_e[slot_of(0, -1)] + recv_e[slot_of(1, -1)]
    right = recv_e[slot_of(-1, 1)] + recv_e[slot_of(0, 1)] + recv_e[slot_of(1, 1)]
    total = total + jnp.where(elane < 2 * m, pltpu.roll(left, LANES - tw, axis=1), 0.0)
    total = total + jnp.where(
        jnp.logical_and(elane >= tw, elane < ew), pltpu.roll(right, tw, axis=1), 0.0
    )
    recon = (total + vb_ref[0]).astype(bf16).astype(f32)
    lo_r = jnp.where(row_at == 0, m, 0)
    hi_r = jnp.where(row_at == n_row - 1, m + th, eh)
    lo_c = jnp.where(col_at == 0, m, 0)
    hi_c = jnp.where(col_at == n_col - 1, m + tw, ew)
    inside = (erow >= lo_r) & (erow < hi_r) & (elane >= lo_c) & (elane < hi_c)
    ext[...] = jnp.where(inside, recon, 0.0)
    own = ext[m : m + th, :]
    for n in range(ni):
        recon_ref[n] = own[:, n * stride + m : n * stride + m + tw].astype(bf16)
    mine = jnp.logical_and(lane >= m, lane < m + tw)
    visible = jnp.sum(jnp.where(mine, pf[...] - own, 0.0))
    place(rows)

    a_neg = a_ref[rows : 2 * rows, :].astype(bf16)
    for b0 in range(0, blocks * LANES, step):
        xw = jnp.dot(a_neg, tz[:, b0 : b0 + step], preferred_element_type=f32)
        for o in range(0, step, LANES):
            at = b0 + o
            e = jnp.exp(xw[:, o : o + LANES] + bias)
            prob = e / pooled(e)
            hidden = hidden - fold(prob)
            h_ref[rows : 2 * rows, at : at + LANES] = (-prob).astype(bf16)

    a_all = a_ref[...].astype(bf16)
    q_len = acc_ref.shape[0]
    acc = None
    for b0 in range(0, blocks * LANES, step):
        g_ref[...] = lax.dot_general(
            a_all, h_ref[:, b0 : b0 + step], (((0,), (0,)), ((), ())), preferred_element_type=f32
        )
        for o in range(0, step, LANES):
            sh = per * ((b0 + o) // LANES)
            part = g_ref[sh : sh + q_len, o : o + LANES]
            acc = part if acc is None else acc + part
    acc_ref[...] = acc
    half = -(-filt // per)
    c_ref[...] = jnp.zeros_like(c_ref)
    for r in range(filt):
        piece = acc_ref[r * ew : r * ew + filt, 0:k]
        for jp in range(1, per):
            piece = piece + acc_ref[r * ew + jp : r * ew + jp + filt, jp * k : (jp + 1) * k]
        at, rr = r // half, r % half
        c_ref[rr * filt : (rr + 1) * filt, at * k : (at + 1) * k] = piece
    hid = jnp.sum(hidden, axis=0, keepdims=True)
    hid = hid + pltpu.roll(hid, LANES // 2, axis=1)
    lane1 = lax.broadcasted_iota(jnp.int32, (1, LANES), 1)
    c_ref[half * filt : half * filt + 1, :] = jnp.where(lane1 < k, hid, jnp.where(lane1 == k, visible, 0.0))

    recv1[me1] = c_ref[...]

    def all_sum(buf, me, size, group, ssem, rsem):
        def copy(d, start):
            other, dev = group(d if start else size - d)
            at = me if start else other
            return pltpu.make_async_remote_copy(
                src_ref=buf.at[me], dst_ref=buf.at[at], send_sem=ssem.at[d], recv_sem=rsem.at[at],
                device_id=dev, device_id_type=MESH,
            )

        for d in range(1, size):
            copy(d, True).start()
        for d in range(1, size):
            copy(d, True).wait_send()
            copy(d, False).wait_recv()
        out = buf[0]
        for i in range(1, size):
            out = out + buf[i]
        return out

    recv2[me2] = all_sum(recv1, me1, n1, group1, s1_sem, r1_sem)
    scale = 1.0 / float(ni * th * tw * n_img * n_row * n_col)
    c_out_ref[...] = all_sum(recv2, me2, n2, group2, s2_sem, r2_sem) * scale


def body(images, filters, hidden_bias, visible_unit_bias, unit_noise):
    ni, th, tw = images.shape
    k, filt, _ = filters.shape
    m = filt // 2
    eh, ew = th + 2 * m, tw + 2 * m
    n_img, n_row, n_col = lax.axis_size("img"), lax.axis_size("row"), lax.axis_size("col")
    rows, wide = ni * th, tw * k
    q = filt * ew
    kp = -(-q // LANES) * LANES
    per = LANES // k
    half = -(-filt // per)
    c_rows = -(-(half * filt + 1) // 8) * 8
    q_len = -(-((filt - 1) * ew + filt + per) // 8) * 8
    top = -(-tw // 16) * 16
    step = 2 * LANES if (wide // LANES) % 2 == 0 else LANES
    fil = jnp.pad(filters.transpose(1, 2, 0), ((0, 0), (0, ew - filt), (0, 0))).reshape(q, k)
    n1, n2 = n_img * n_row, n_col
    vmem = pl.BlockSpec(memory_space=pltpu.VMEM)
    recon, c = pl.pallas_call(
        functools.partial(kernel, (ni, th, tw, k, filt, n_img, n_row, n_col)),
        out_shape=(
            jax.ShapeDtypeStruct((ni, th, tw), bf16),
            jax.ShapeDtypeStruct((c_rows, LANES), f32),
        ),
        in_specs=[vmem, vmem, vmem, pl.BlockSpec(memory_space=pltpu.SMEM), vmem],
        out_specs=(vmem, vmem),
        scratch_shapes=[
            pltpu.VMEM((th, LANES), f32),
            pltpu.VMEM((th, LANES), bf16),
            pltpu.VMEM((9, th, LANES), bf16),
            pltpu.VMEM((eh, LANES), f32),
            pltpu.VMEM((2 * rows, kp), f32),
            pltpu.VMEM((top + kp, LANES), f32),
            pltpu.VMEM((kp, wide), bf16),
            pltpu.VMEM((rows, wide), f32),
            pltpu.VMEM((2 * rows, wide), bf16),
            pltpu.VMEM((rows, wide), bf16),
            pltpu.VMEM((rows, kp), f32),
            pltpu.VMEM((eh, LANES), f32),
            pltpu.VMEM((9, eh, LANES), f32),
            pltpu.VMEM((kp, step), f32),
            pltpu.VMEM((q_len, LANES), f32),
            pltpu.VMEM((c_rows, LANES), f32),
            pltpu.VMEM((n1, c_rows, LANES), f32),
            pltpu.VMEM((n2, c_rows, LANES), f32),
            pltpu.SemaphoreType.DMA((9,)),
            pltpu.SemaphoreType.DMA((9,)),
            pltpu.SemaphoreType.DMA((9,)),
            pltpu.SemaphoreType.DMA((9,)),
            pltpu.SemaphoreType.DMA((n1,)),
            pltpu.SemaphoreType.DMA((n1,)),
            pltpu.SemaphoreType.DMA((n2,)),
            pltpu.SemaphoreType.DMA((n2,)),
        ],
        compiler_params=pltpu.CompilerParams(collective_id=0, has_side_effects=True),
    )(
        images,
        fil,
        hidden_bias.reshape(1, k),
        visible_unit_bias.reshape(1),
        unit_noise.reshape(rows, wide),
    )
    parts = c[: half * filt].reshape(half, filt, per, k)
    grad = parts.transpose(3, 2, 0, 1).reshape(k, per * half, filt)[:, :filt]
    return recon, grad, c[half * filt, :k], c[half * filt, k]


def solution(mesh):
    in_specs = (P("img", "row", "col"), P(), P(), P(), P("img", "row", "col"))
    out_specs = (P("img", "row", "col"), P(), P(), P())
    return jax.shard_map(body, mesh=mesh, in_specs=in_specs, out_specs=out_specs, check_vma=False)
```

```python
import functools

import jax
import jax.numpy as jnp
from jax import lax
from jax.experimental import pallas as pl
from jax.experimental.pallas import tpu as pltpu
from jax.sharding import PartitionSpec as P

LANES = 128
MESH = pl.DeviceIdType.MESH
DIRS = [(dr, dc) for dr in (-1, 0, 1) for dc in (-1, 0, 1) if (dr, dc) != (0, 0)]
f32 = jnp.float32
bf16 = jnp.bfloat16


def slot_of(dr, dc):
    return (dr + 1) * 3 + dc + 1


def pooled(e):
    rows = e.shape[0]
    s = e + pltpu.roll(e, LANES // 2, axis=1)
    s3 = s.reshape(rows // 8, 8, LANES)
    even = lax.broadcasted_iota(jnp.int32, s3.shape, 1) % 2 == 0
    t3 = jnp.where(even, pltpu.roll(s3, 7, axis=1), pltpu.roll(s3, 1, axis=1))
    return 1.0 + s + t3.reshape(rows, LANES)


def kernel(
    geo, img_hbm, fil_hbm, hb_hbm, vb_hbm, noise_hbm, recon_hbm, grad_ref, gh_ref, gv_ref,
    img_ref, fil_ref, hb_ref, vb_ref, noise_ref, recon_ref, in_sem, out_sem, pf, pack, recv_img, ext, a_ref, fp, tz, w_ref, h_ref, s_ref, u_ref, e_ref, recv_e,
    g_ref, acc_ref, c_ref, recv1, recv2, is_sem, ir_sem, es_sem, er_sem, s1_sem, r1_sem, s2_sem, r2_sem,
):
    ni, th, tw, k, filt, n_img, n_row, n_col = geo
    m = filt // 2
    eh, ew = th + 2 * m, tw + 2 * m
    stride = LANES // ni
    rows = ni * th
    blocks = tw * k // LANES
    kp = a_ref.shape[1]
    img_at, row_at, col_at = lax.axis_index("img"), lax.axis_index("row"), lax.axis_index("col")
    n1, n2 = n_img * n_row, n_col
    me1, me2 = img_at * n_row + row_at, col_at

    def exists(dr, dc):
        ok = True
        if dr:
            ok = (row_at > 0) if dr < 0 else (row_at < n_row - 1)
        if dc:
            ok2 = (col_at > 0) if dc < 0 else (col_at < n_col - 1)
            ok = jnp.logical_and(ok, ok2) if dr else ok2
        return ok

    def neighbour(dr, dc):
        return {"row": row_at + dr, "col": col_at + dc}

    def group1(d):
        other = lax.rem(me1 + d, n1)
        return other, {"img": other // n_row, "row": lax.rem(other, n_row)}

    def group2(d):
        other = lax.rem(me2 + d, n2)
        return other, {"col": other}

    loads = [
        pltpu.make_async_copy(src, dst, in_sem.at[i])
        for i, (src, dst) in enumerate(
            [(img_hbm, img_ref), (fil_hbm, fil_ref), (noise_hbm, noise_ref), (hb_hbm, hb_ref), (vb_hbm, vb_ref)]
        )
    ]
    for load in loads:
        load.start()

    recv_img[...] = jnp.zeros_like(recv_img)
    recv_e[...] = jnp.zeros_like(recv_e)
    barrier = pltpu.get_barrier_semaphore()
    count = jnp.int32(n1 - 1 + n2 - 1)
    for d in DIRS:
        @pl.when(exists(*d))
        def _(d=d):
            pl.semaphore_signal(barrier, inc=1, device_id=neighbour(*d), device_id_type=MESH)
        count = count + exists(*d).astype(jnp.int32)
    for d in range(1, n1):
        pl.semaphore_signal(barrier, inc=1, device_id=group1(d)[1], device_id_type=MESH)
    for d in range(1, n2):
        pl.semaphore_signal(barrier, inc=1, device_id=group2(d)[1], device_id_type=MESH)

    pf[...] = jnp.zeros_like(pf)
    fp[...] = jnp.zeros_like(fp)
    a_ref[...] = jnp.zeros_like(a_ref)
    loads[0].wait()
    for n in range(ni):
        pf[:, n * stride + m : n * stride + m + tw] = img_ref[n].astype(f32)
    pack[...] = pf[...].astype(bf16)

    top = fp.shape[0] - kp
    per = LANES // k
    loads[1].wait()
    for r in range(filt):
        fv = fil_ref[r].astype(f32)
        for jp in range(per):
            fp[top + jp + r * ew : top + jp + r * ew + filt, jp * k : (jp + 1) * k] = fv
    pl.semaphore_wait(barrier, count)

    def img_copy(dr, dc, start):
        at = slot_of(-dr, -dc) if start else slot_of(dr, dc)
        return pltpu.make_async_remote_copy(
            src_ref=pack, dst_ref=recv_img.at[at], send_sem=is_sem.at[at], recv_sem=ir_sem.at[at],
            device_id=neighbour(dr, dc), device_id_type=MESH,
        )

    for d in DIRS:
        @pl.when(exists(*d))
        def _(d=d):
            img_copy(*d, True).start()

    loads[2].wait()
    loads[3].wait()
    loads[4].wait()
    for b in range(blocks):
        tz[:, b * LANES : (b + 1) * LANES] = fp[top - per * b : top - per * b + kp, :].astype(bf16)
        w_ref[:, b * LANES : (b + 1) * LANES] = 1.0 / jnp.log(noise_ref[:, b * LANES : (b + 1) * LANES].astype(f32))

    lane = lax.broadcasted_iota(jnp.int32, (th, LANES), 1) % stride

    def place(a_row):
        for n in range(ni):
            for r in range(filt):
                a_ref[a_row + n * th : a_row + (n + 1) * th, r * ew : (r + 1) * ew] = ext[
                    r : r + th, n * stride : n * stride + ew
                ]

    for d in DIRS:
        @pl.when(exists(*d))
        def _(d=d):
            img_copy(*d, True).wait_send()
            img_copy(*d, False).wait_recv()

    for dr in (-1, 0, 1):
        centre = pf[...] if dr == 0 else recv_img[slot_of(dr, 0)].astype(f32)
        left = pltpu.roll(recv_img[slot_of(dr, -1)].astype(f32), LANES - tw, axis=1)
        right = pltpu.roll(recv_img[slot_of(dr, 1)].astype(f32), tw, axis=1)
        band = jnp.where(lane < m, left, jnp.where(lane < m + tw, centre, jnp.where(lane < ew, right, 0.0)))
        if dr == 0:
            ext[m : m + th, :] = band
        elif dr < 0:
            ext[0:m, :] = band[th - m :, :]
        else:
            ext[m + th :, :] = band[:m, :]
    place(0)

    bias = jnp.concatenate([hb_ref[...]] * per, axis=1)
    a_pos = a_ref[0:rows, :].astype(bf16)
    hidden = jnp.zeros((8, LANES), f32)

    def fold(x):
        return jnp.sum(x.reshape(rows // 8, 8, LANES), axis=0)

    step = 2 * LANES if blocks % 2 == 0 else LANES
    for b0 in range(0, blocks * LANES, step):
        xw = jnp.dot(a_pos, tz[:, b0 : b0 + step], preferred_element_type=f32)
        for o in range(0, step, LANES):
            at = b0 + o
            e = jnp.exp(xw[:, o : o + LANES] + bias)
            prob = e / pooled(e)
            hidden = hidden + fold(prob)
            h_ref[0:rows, at : at + LANES] = prob.astype(bf16)
            t = e * w_ref[:, at : at + LANES]
            t = t * t
            s_ref[:, at : at + LANES] = (t / pooled(t)).astype(bf16)

    u_ref[...] = lax.dot_general(s_ref[...], tz[...], (((1,), (1,)), ((), ())), preferred_element_type=f32)
    e_ref[...] = jnp.zeros_like(e_ref)
    gap = jnp.zeros((th, stride - ew), f32)
    for r in range(filt):
        pieces = []
        for n in range(ni):
            pieces += [u_ref[n * th : (n + 1) * th, r * ew : (r + 1) * ew], gap]
        e_ref[r : r + th, :] += jnp.concatenate(pieces, axis=1)

    def e_copy(dr, dc, start):
        at = slot_of(-dr, -dc) if start else slot_of(dr, dc)
        way = dr if start else -dr
        if way == 0:
            src, dst = e_ref, recv_e.at[at]
        elif way > 0:
            src, dst = e_ref.at[th:eh], recv_e.at[at, 0 : 2 * m]
        else:
            src, dst = e_ref.at[0 : 2 * m], recv_e.at[at, th:eh]
        return pltpu.make_async_remote_copy(
            src_ref=src, dst_ref=dst, send_sem=es_sem.at[at], recv_sem=er_sem.at[at],
            device_id=neighbour(dr, dc), device_id_type=MESH,
        )

    for d in DIRS:
        @pl.when(exists(*d))
        def _(d=d):
            e_copy(*d, True).start()
    for d in DIRS:
        @pl.when(exists(*d))
        def _(d=d):
            e_copy(*d, True).wait_send()
            e_copy(*d, False).wait_recv()

    elane = lax.broadcasted_iota(jnp.int32, (eh, LANES), 1) % stride
    erow = lax.broadcasted_iota(jnp.int32, (eh, LANES), 0)
    total = e_ref[...] + recv_e[slot_of(-1, 0)] + recv_e[slot_of(1, 0)]
    left = recv_e[slot_of(-1, -1)] + recv_e[slot_of(0, -1)] + recv_e[slot_of(1, -1)]
    right = recv_e[slot_of(-1, 1)] + recv_e[slot_of(0, 1)] + recv_e[slot_of(1, 1)]
    total = total + jnp.where(elane < 2 * m, pltpu.roll(left, LANES - tw, axis=1), 0.0)
    total = total + jnp.where(
        jnp.logical_and(elane >= tw, elane < ew), pltpu.roll(right, tw, axis=1), 0.0
    )
    recon = (total + vb_ref[...]).astype(bf16).astype(f32)
    lo_r = jnp.where(row_at == 0, m, 0)
    hi_r = jnp.where(row_at == n_row - 1, m + th, eh)
    lo_c = jnp.where(col_at == 0, m, 0)
    hi_c = jnp.where(col_at == n_col - 1, m + tw, ew)
    inside = (erow >= lo_r) & (erow < hi_r) & (elane >= lo_c) & (elane < hi_c)
    ext[...] = jnp.where(inside, recon, 0.0)
    own = ext[m : m + th, :]
    for n in range(ni):
        recon_ref[n] = own[:, n * stride + m : n * stride + m + tw].astype(bf16)
    out_copy = pltpu.make_async_copy(recon_ref, recon_hbm, out_sem)
    out_copy.start()
    mine = jnp.logical_and(lane >= m, lane < m + tw)
    visible = jnp.sum(jnp.where(mine, pf[...] - own, 0.0))
    place(rows)

    a_neg = a_ref[rows : 2 * rows, :].astype(bf16)
    for b0 in range(0, blocks * LANES, step):
        xw = jnp.dot(a_neg, tz[:, b0 : b0 + step], preferred_element_type=f32)
        for o in range(0, step, LANES):
            at = b0 + o
            e = jnp.exp(xw[:, o : o + LANES] + bias)
            prob = e / pooled(e)
            hidden = hidden - fold(prob)
            h_ref[rows : 2 * rows, at : at + LANES] = (-prob).astype(bf16)

    a_all = a_ref[...].astype(bf16)
    q_len = acc_ref.shape[0]
    acc = None
    for b0 in range(0, blocks * LANES, step):
        g_ref[...] = lax.dot_general(
            a_all, h_ref[:, b0 : b0 + step], (((0,), (0,)), ((), ())), preferred_element_type=f32
        )
        for o in range(0, step, LANES):
            sh = per * ((b0 + o) // LANES)
            part = g_ref[sh : sh + q_len, o : o + LANES]
            acc = part if acc is None else acc + part
    acc_ref[...] = acc
    half = -(-filt // per)
    c_ref[...] = jnp.zeros_like(c_ref)
    for r in range(filt):
        piece = acc_ref[r * ew : r * ew + filt, 0:k]
        for jp in range(1, per):
            piece = piece + acc_ref[r * ew + jp : r * ew + jp + filt, jp * k : (jp + 1) * k]
        at, rr = r // half, r % half
        c_ref[rr * filt : (rr + 1) * filt, at * k : (at + 1) * k] = piece
    hid = jnp.sum(hidden, axis=0, keepdims=True)
    hid = hid + pltpu.roll(hid, LANES // 2, axis=1)
    lane1 = lax.broadcasted_iota(jnp.int32, (1, LANES), 1)
    c_ref[half * filt : half * filt + 1, :] = jnp.where(lane1 < k, hid, jnp.where(lane1 == k, visible, 0.0))

    recv1[me1] = c_ref[...]

    def all_sum(buf, me, size, group, ssem, rsem):
        def copy(d, start):
            other, dev = group(d if start else size - d)
            at = me if start else other
            return pltpu.make_async_remote_copy(
                src_ref=buf.at[me], dst_ref=buf.at[at], send_sem=ssem.at[d], recv_sem=rsem.at[at],
                device_id=dev, device_id_type=MESH,
            )

        for d in range(1, size):
            copy(d, True).start()
        for d in range(1, size):
            copy(d, True).wait_send()
            copy(d, False).wait_recv()
        out = buf[0]
        for i in range(1, size):
            out = out + buf[i]
        return out

    recv2[me2] = all_sum(recv1, me1, n1, group1, s1_sem, r1_sem)
    scale = 1.0 / float(ni * th * tw * n_img * n_row * n_col)
    final = all_sum(recv2, me2, n2, group2, s2_sem, r2_sem) * scale
    c_ref[...] = final
    for r in range(filt):
        at, rr = r // half, r % half
        grad_ref[r] = c_ref[rr * filt : (rr + 1) * filt, at * k : (at + 1) * k]
    gh_ref[...] = c_ref[half * filt : half * filt + 1, 0:k]
    gv_ref[...] = c_ref[half * filt : half * filt + 1, k : k + 1]
    out_copy.wait()


def body(images, filters, hidden_bias, visible_unit_bias, unit_noise):
    ni, th, tw = images.shape
    k, filt, _ = filters.shape
    m = filt // 2
    eh, ew = th + 2 * m, tw + 2 * m
    n_img, n_row, n_col = lax.axis_size("img"), lax.axis_size("row"), lax.axis_size("col")
    rows, wide = ni * th, tw * k
    q = filt * ew
    kp = -(-q // LANES) * LANES
    per = LANES // k
    half = -(-filt // per)
    c_rows = -(-(half * filt + 1) // 8) * 8
    q_len = -(-((filt - 1) * ew + filt + per) // 8) * 8
    top = -(-tw // 16) * 16
    step = 2 * LANES if (wide // LANES) % 2 == 0 else LANES
    n1, n2 = n_img * n_row, n_col
    vmem = pl.BlockSpec(memory_space=pltpu.VMEM)
    hbm = pl.BlockSpec(memory_space=pl.ANY)
    recon, grad, grad_hidden, grad_visible = pl.pallas_call(
        functools.partial(kernel, (ni, th, tw, k, filt, n_img, n_row, n_col)),
        out_shape=(
            jax.ShapeDtypeStruct((ni, th, tw), bf16),
            jax.ShapeDtypeStruct((filt, filt, k), f32),
            jax.ShapeDtypeStruct((1, k), f32),
            jax.ShapeDtypeStruct((1, 1), f32),
        ),
        in_specs=[hbm] * 5,
        out_specs=(hbm, vmem, vmem, vmem),
        scratch_shapes=[
            pltpu.VMEM((ni, th, tw), bf16),
            pltpu.VMEM((filt, filt, k), bf16),
            pltpu.VMEM((1, k), f32),
            pltpu.VMEM((1, 1), f32),
            pltpu.VMEM((rows, wide), bf16),
            pltpu.VMEM((ni, th, tw), bf16),
            pltpu.SemaphoreType.DMA((5,)),
            pltpu.SemaphoreType.DMA,
            pltpu.VMEM((th, LANES), f32),
            pltpu.VMEM((th, LANES), bf16),
            pltpu.VMEM((9, th, LANES), bf16),
            pltpu.VMEM((eh, LANES), f32),
            pltpu.VMEM((2 * rows, kp), f32),
            pltpu.VMEM((top + kp, LANES), f32),
            pltpu.VMEM((kp, wide), bf16),
            pltpu.VMEM((rows, wide), f32),
            pltpu.VMEM((2 * rows, wide), bf16),
            pltpu.VMEM((rows, wide), bf16),
            pltpu.VMEM((rows, kp), f32),
            pltpu.VMEM((eh, LANES), f32),
            pltpu.VMEM((9, eh, LANES), f32),
            pltpu.VMEM((kp, step), f32),
            pltpu.VMEM((q_len, LANES), f32),
            pltpu.VMEM((c_rows, LANES), f32),
            pltpu.VMEM((n1, c_rows, LANES), f32),
            pltpu.VMEM((n2, c_rows, LANES), f32),
            pltpu.SemaphoreType.DMA((9,)),
            pltpu.SemaphoreType.DMA((9,)),
            pltpu.SemaphoreType.DMA((9,)),
            pltpu.SemaphoreType.DMA((9,)),
            pltpu.SemaphoreType.DMA((n1,)),
            pltpu.SemaphoreType.DMA((n1,)),
            pltpu.SemaphoreType.DMA((n2,)),
            pltpu.SemaphoreType.DMA((n2,)),
        ],
        compiler_params=pltpu.CompilerParams(collective_id=0, has_side_effects=True),
    )(
        images,
        filters.transpose(1, 2, 0),
        hidden_bias.reshape(1, k),
        visible_unit_bias.reshape(1, 1),
        unit_noise.reshape(rows, wide),
    )
    return recon, grad.transpose(2, 0, 1), grad_hidden.reshape(k), grad_visible.reshape(())


def solution(mesh):
    in_specs = (P("img", "row", "col"), P(), P(), P(), P("img", "row", "col"))
    out_specs = (P("img", "row", "col"), P(), P(), P())
    return jax.shard_map(body, mesh=mesh, in_specs=in_specs, out_specs=out_specs, check_vma=False)
```

```python
import functools

import jax
import jax.numpy as jnp
from jax import lax
from jax.experimental import pallas as pl
from jax.experimental.pallas import tpu as pltpu
from jax.sharding import PartitionSpec as P

LANES = 128
MESH = pl.DeviceIdType.MESH
DIRS = [(dr, dc) for dr in (-1, 0, 1) for dc in (-1, 0, 1) if (dr, dc) != (0, 0)]
f32 = jnp.float32
bf16 = jnp.bfloat16


def slot_of(dr, dc):
    return (dr + 1) * 3 + dc + 1


def pooled(e):
    rows = e.shape[0]
    s = e + pltpu.roll(e, LANES // 2, axis=1)
    s3 = s.reshape(rows // 8, 8, LANES)
    even = lax.broadcasted_iota(jnp.int32, s3.shape, 1) % 2 == 0
    t3 = jnp.where(even, pltpu.roll(s3, 7, axis=1), pltpu.roll(s3, 1, axis=1))
    return 1.0 + s + t3.reshape(rows, LANES)


def kernel(
    geo, img_hbm, fil_hbm, hb_hbm, vb_hbm, noise_hbm, recon_hbm, c_out_ref,
    img_ref, fil_ref, hb_ref, vb_ref, noise_ref, recon_ref, in_sem, out_sem, pf, pack, recv_img, ext, a_ref, fp, tz, w_ref, h_ref, s_ref, u_ref, e_ref, recv_e,
    g_ref, acc_ref, c_ref, recv1, recv2, is_sem, ir_sem, es_sem, er_sem, s1_sem, r1_sem, s2_sem, r2_sem,
):
    ni, th, tw, k, filt, n_img, n_row, n_col = geo
    m = filt // 2
    eh, ew = th + 2 * m, tw + 2 * m
    stride = LANES // ni
    rows = ni * th
    blocks = tw * k // LANES
    kp = a_ref.shape[1]
    img_at, row_at, col_at = lax.axis_index("img"), lax.axis_index("row"), lax.axis_index("col")
    n1, n2 = n_img * n_row, n_col
    me1, me2 = img_at * n_row + row_at, col_at

    def exists(dr, dc):
        ok = True
        if dr:
            ok = (row_at > 0) if dr < 0 else (row_at < n_row - 1)
        if dc:
            ok2 = (col_at > 0) if dc < 0 else (col_at < n_col - 1)
            ok = jnp.logical_and(ok, ok2) if dr else ok2
        return ok

    def neighbour(dr, dc):
        return {"row": row_at + dr, "col": col_at + dc}

    def group1(d):
        other = lax.rem(me1 + d, n1)
        return other, {"img": other // n_row, "row": lax.rem(other, n_row)}

    def group2(d):
        other = lax.rem(me2 + d, n2)
        return other, {"col": other}

    loads = [
        pltpu.make_async_copy(src, dst, in_sem.at[i])
        for i, (src, dst) in enumerate(
            [(img_hbm, img_ref), (fil_hbm, fil_ref), (noise_hbm, noise_ref), (hb_hbm, hb_ref), (vb_hbm, vb_ref)]
        )
    ]
    for load in loads:
        load.start()

    recv_img[...] = jnp.zeros_like(recv_img)
    recv_e[...] = jnp.zeros_like(recv_e)
    barrier = pltpu.get_barrier_semaphore()
    count = jnp.int32(n1 - 1 + n2 - 1)
    for d in DIRS:
        @pl.when(exists(*d))
        def _(d=d):
            pl.semaphore_signal(barrier, inc=1, device_id=neighbour(*d), device_id_type=MESH)
        count = count + exists(*d).astype(jnp.int32)
    for d in range(1, n1):
        pl.semaphore_signal(barrier, inc=1, device_id=group1(d)[1], device_id_type=MESH)
    for d in range(1, n2):
        pl.semaphore_signal(barrier, inc=1, device_id=group2(d)[1], device_id_type=MESH)

    pf[...] = jnp.zeros_like(pf)
    fp[...] = jnp.zeros_like(fp)
    a_ref[...] = jnp.zeros_like(a_ref)
    loads[0].wait()
    for n in range(ni):
        pf[:, n * stride + m : n * stride + m + tw] = img_ref[n].astype(f32)
    pack[...] = pf[...].astype(bf16)

    top = fp.shape[0] - kp
    per = LANES // k
    loads[1].wait()
    for r in range(filt):
        fv = fil_ref[r].astype(f32)
        for jp in range(per):
            fp[top + jp + r * ew : top + jp + r * ew + filt, jp * k : (jp + 1) * k] = fv
    pl.semaphore_wait(barrier, count)

    def img_copy(dr, dc, start):
        at = slot_of(-dr, -dc) if start else slot_of(dr, dc)
        return pltpu.make_async_remote_copy(
            src_ref=pack, dst_ref=recv_img.at[at], send_sem=is_sem.at[at], recv_sem=ir_sem.at[at],
            device_id=neighbour(dr, dc), device_id_type=MESH,
        )

    for d in DIRS:
        @pl.when(exists(*d))
        def _(d=d):
            img_copy(*d, True).start()

    loads[2].wait()
    loads[3].wait()
    loads[4].wait()
    for b in range(blocks):
        tz[:, b * LANES : (b + 1) * LANES] = fp[top - per * b : top - per * b + kp, :].astype(bf16)
        w_ref[:, b * LANES : (b + 1) * LANES] = 1.0 / jnp.log(noise_ref[:, b * LANES : (b + 1) * LANES].astype(f32))

    lane = lax.broadcasted_iota(jnp.int32, (th, LANES), 1) % stride

    def place(a_row):
        for n in range(ni):
            for r in range(filt):
                a_ref[a_row + n * th : a_row + (n + 1) * th, r * ew : (r + 1) * ew] = ext[
                    r : r + th, n * stride : n * stride + ew
                ]

    for d in DIRS:
        @pl.when(exists(*d))
        def _(d=d):
            img_copy(*d, True).wait_send()
            img_copy(*d, False).wait_recv()

    for dr in (-1, 0, 1):
        centre = pf[...] if dr == 0 else recv_img[slot_of(dr, 0)].astype(f32)
        left = pltpu.roll(recv_img[slot_of(dr, -1)].astype(f32), LANES - tw, axis=1)
        right = pltpu.roll(recv_img[slot_of(dr, 1)].astype(f32), tw, axis=1)
        band = jnp.where(lane < m, left, jnp.where(lane < m + tw, centre, jnp.where(lane < ew, right, 0.0)))
        if dr == 0:
            ext[m : m + th, :] = band
        elif dr < 0:
            ext[0:m, :] = band[th - m :, :]
        else:
            ext[m + th :, :] = band[:m, :]
    place(0)

    bias = jnp.concatenate([hb_ref[...]] * per, axis=1)
    a_pos = a_ref[0:rows, :].astype(bf16)
    hidden = jnp.zeros((8, LANES), f32)

    def fold(x):
        return jnp.sum(x.reshape(rows // 8, 8, LANES), axis=0)

    step = 2 * LANES if blocks % 2 == 0 else LANES
    for b0 in range(0, blocks * LANES, step):
        xw = jnp.dot(a_pos, tz[:, b0 : b0 + step], preferred_element_type=f32)
        for o in range(0, step, LANES):
            at = b0 + o
            e = jnp.exp(xw[:, o : o + LANES] + bias)
            prob = e / pooled(e)
            hidden = hidden + fold(prob)
            h_ref[0:rows, at : at + LANES] = prob.astype(bf16)
            t = e * w_ref[:, at : at + LANES]
            t = t * t
            s_ref[:, at : at + LANES] = (t / pooled(t)).astype(bf16)

    u_ref[...] = lax.dot_general(s_ref[...], tz[...], (((1,), (1,)), ((), ())), preferred_element_type=f32)
    e_ref[...] = jnp.zeros_like(e_ref)
    gap = jnp.zeros((th, stride - ew), f32)
    for r in range(filt):
        pieces = []
        for n in range(ni):
            pieces += [u_ref[n * th : (n + 1) * th, r * ew : (r + 1) * ew], gap]
        e_ref[r : r + th, :] += jnp.concatenate(pieces, axis=1)

    def e_copy(dr, dc, start):
        at = slot_of(-dr, -dc) if start else slot_of(dr, dc)
        way = dr if start else -dr
        if way == 0:
            src, dst = e_ref, recv_e.at[at]
        elif way > 0:
            src, dst = e_ref.at[th:eh], recv_e.at[at, 0 : 2 * m]
        else:
            src, dst = e_ref.at[0 : 2 * m], recv_e.at[at, th:eh]
        return pltpu.make_async_remote_copy(
            src_ref=src, dst_ref=dst, send_sem=es_sem.at[at], recv_sem=er_sem.at[at],
            device_id=neighbour(dr, dc), device_id_type=MESH,
        )

    for d in DIRS:
        @pl.when(exists(*d))
        def _(d=d):
            e_copy(*d, True).start()
    for d in DIRS:
        @pl.when(exists(*d))
        def _(d=d):
            e_copy(*d, True).wait_send()
            e_copy(*d, False).wait_recv()

    elane = lax.broadcasted_iota(jnp.int32, (eh, LANES), 1) % stride
    erow = lax.broadcasted_iota(jnp.int32, (eh, LANES), 0)
    total = e_ref[...] + recv_e[slot_of(-1, 0)] + recv_e[slot_of(1, 0)]
    left = recv_e[slot_of(-1, -1)] + recv_e[slot_of(0, -1)] + recv_e[slot_of(1, -1)]
    right = recv_e[slot_of(-1, 1)] + recv_e[slot_of(0, 1)] + recv_e[slot_of(1, 1)]
    total = total + jnp.where(elane < 2 * m, pltpu.roll(left, LANES - tw, axis=1), 0.0)
    total = total + jnp.where(
        jnp.logical_and(elane >= tw, elane < ew), pltpu.roll(right, tw, axis=1), 0.0
    )
    recon = (total + vb_ref[...]).astype(bf16).astype(f32)
    lo_r = jnp.where(row_at == 0, m, 0)
    hi_r = jnp.where(row_at == n_row - 1, m + th, eh)
    lo_c = jnp.where(col_at == 0, m, 0)
    hi_c = jnp.where(col_at == n_col - 1, m + tw, ew)
    inside = (erow >= lo_r) & (erow < hi_r) & (elane >= lo_c) & (elane < hi_c)
    ext[...] = jnp.where(inside, recon, 0.0)
    own = ext[m : m + th, :]
    for n in range(ni):
        recon_ref[n] = own[:, n * stride + m : n * stride + m + tw].astype(bf16)
    out_copy = pltpu.make_async_copy(recon_ref, recon_hbm, out_sem)
    out_copy.start()
    mine = jnp.logical_and(lane >= m, lane < m + tw)
    visible = jnp.sum(jnp.where(mine, pf[...] - own, 0.0))
    place(rows)

    a_neg = a_ref[rows : 2 * rows, :].astype(bf16)
    for b0 in range(0, blocks * LANES, step):
        xw = jnp.dot(a_neg, tz[:, b0 : b0 + step], preferred_element_type=f32)
        for o in range(0, step, LANES):
            at = b0 + o
            e = jnp.exp(xw[:, o : o + LANES] + bias)
            prob = e / pooled(e)
            hidden = hidden - fold(prob)
            h_ref[rows : 2 * rows, at : at + LANES] = (-prob).astype(bf16)

    a_all = a_ref[...].astype(bf16)
    q_len = acc_ref.shape[0]
    acc = None
    for b0 in range(0, blocks * LANES, step):
        g_ref[...] = lax.dot_general(
            a_all, h_ref[:, b0 : b0 + step], (((0,), (0,)), ((), ())), preferred_element_type=f32
        )
        for o in range(0, step, LANES):
            sh = per * ((b0 + o) // LANES)
            part = g_ref[sh : sh + q_len, o : o + LANES]
            acc = part if acc is None else acc + part
    acc_ref[...] = acc
    half = -(-filt // per)
    c_ref[...] = jnp.zeros_like(c_ref)
    for r in range(filt):
        piece = acc_ref[r * ew : r * ew + filt, 0:k]
        for jp in range(1, per):
            piece = piece + acc_ref[r * ew + jp : r * ew + jp + filt, jp * k : (jp + 1) * k]
        at, rr = r // half, r % half
        c_ref[rr * filt : (rr + 1) * filt, at * k : (at + 1) * k] = piece
    hid = jnp.sum(hidden, axis=0, keepdims=True)
    hid = hid + pltpu.roll(hid, LANES // 2, axis=1)
    lane1 = lax.broadcasted_iota(jnp.int32, (1, LANES), 1)
    c_ref[half * filt : half * filt + 1, :] = jnp.where(lane1 < k, hid, jnp.where(lane1 == k, visible, 0.0))

    recv1[me1] = c_ref[...]

    def all_sum(buf, me, size, group, ssem, rsem):
        def copy(d, start):
            other, dev = group(d if start else size - d)
            at = me if start else other
            return pltpu.make_async_remote_copy(
                src_ref=buf.at[me], dst_ref=buf.at[at], send_sem=ssem.at[d], recv_sem=rsem.at[at],
                device_id=dev, device_id_type=MESH,
            )

        for d in range(1, size):
            copy(d, True).start()
        for d in range(1, size):
            copy(d, True).wait_send()
            copy(d, False).wait_recv()
        out = buf[0]
        for i in range(1, size):
            out = out + buf[i]
        return out

    recv2[me2] = all_sum(recv1, me1, n1, group1, s1_sem, r1_sem)
    scale = 1.0 / float(ni * th * tw * n_img * n_row * n_col)
    c_out_ref[...] = all_sum(recv2, me2, n2, group2, s2_sem, r2_sem) * scale
    out_copy.wait()


def unpack(geo, recon_in, c_ref, recon_ref, grad_ref, gh_ref, gv_ref):
    filt, k = geo
    half = -(-filt // (LANES // k))
    recon_ref[...] = recon_in[...]
    for r in range(filt):
        at, rr = r // half, r % half
        grad_ref[r] = c_ref[rr * filt : (rr + 1) * filt, at * k : (at + 1) * k]
    gh_ref[...] = c_ref[half * filt : half * filt + 1, 0:k]
    gv_ref[...] = c_ref[half * filt : half * filt + 1, k : k + 1]


def body(images, filters, hidden_bias, visible_unit_bias, unit_noise):
    ni, th, tw = images.shape
    k, filt, _ = filters.shape
    m = filt // 2
    eh, ew = th + 2 * m, tw + 2 * m
    n_img, n_row, n_col = lax.axis_size("img"), lax.axis_size("row"), lax.axis_size("col")
    rows, wide = ni * th, tw * k
    q = filt * ew
    kp = -(-q // LANES) * LANES
    per = LANES // k
    half = -(-filt // per)
    c_rows = -(-(half * filt + 1) // 8) * 8
    q_len = -(-((filt - 1) * ew + filt + per) // 8) * 8
    top = -(-tw // 16) * 16
    step = 2 * LANES if (wide // LANES) % 2 == 0 else LANES
    n1, n2 = n_img * n_row, n_col
    vmem = pl.BlockSpec(memory_space=pltpu.VMEM)
    hbm = pl.BlockSpec(memory_space=pl.ANY)
    recon, c = pl.pallas_call(
        functools.partial(kernel, (ni, th, tw, k, filt, n_img, n_row, n_col)),
        out_shape=(
            jax.ShapeDtypeStruct((ni, th, tw), bf16),
            jax.ShapeDtypeStruct((c_rows, LANES), f32),
        ),
        in_specs=[hbm] * 5,
        out_specs=(hbm, vmem),
        scratch_shapes=[
            pltpu.VMEM((ni, th, tw), bf16),
            pltpu.VMEM((filt, filt, k), bf16),
            pltpu.VMEM((1, k), f32),
            pltpu.VMEM((1, 1), f32),
            pltpu.VMEM((rows, wide), bf16),
            pltpu.VMEM((ni, th, tw), bf16),
            pltpu.SemaphoreType.DMA((5,)),
            pltpu.SemaphoreType.DMA,
            pltpu.VMEM((th, LANES), f32),
            pltpu.VMEM((th, LANES), bf16),
            pltpu.VMEM((9, th, LANES), bf16),
            pltpu.VMEM((eh, LANES), f32),
            pltpu.VMEM((2 * rows, kp), f32),
            pltpu.VMEM((top + kp, LANES), f32),
            pltpu.VMEM((kp, wide), bf16),
            pltpu.VMEM((rows, wide), f32),
            pltpu.VMEM((2 * rows, wide), bf16),
            pltpu.VMEM((rows, wide), bf16),
            pltpu.VMEM((rows, kp), f32),
            pltpu.VMEM((eh, LANES), f32),
            pltpu.VMEM((9, eh, LANES), f32),
            pltpu.VMEM((kp, step), f32),
            pltpu.VMEM((q_len, LANES), f32),
            pltpu.VMEM((c_rows, LANES), f32),
            pltpu.VMEM((n1, c_rows, LANES), f32),
            pltpu.VMEM((n2, c_rows, LANES), f32),
            pltpu.SemaphoreType.DMA((9,)),
            pltpu.SemaphoreType.DMA((9,)),
            pltpu.SemaphoreType.DMA((9,)),
            pltpu.SemaphoreType.DMA((9,)),
            pltpu.SemaphoreType.DMA((n1,)),
            pltpu.SemaphoreType.DMA((n1,)),
            pltpu.SemaphoreType.DMA((n2,)),
            pltpu.SemaphoreType.DMA((n2,)),
        ],
        compiler_params=pltpu.CompilerParams(collective_id=0, has_side_effects=True),
    )(
        images,
        filters.transpose(1, 2, 0),
        hidden_bias.reshape(1, k),
        visible_unit_bias.reshape(1, 1),
        unit_noise.reshape(rows, wide),
    )
    recon, grad, grad_hidden, grad_visible = pl.pallas_call(
        functools.partial(unpack, (filt, k)),
        out_shape=(
            jax.ShapeDtypeStruct((ni, th, tw), bf16),
            jax.ShapeDtypeStruct((filt, filt, k), f32),
            jax.ShapeDtypeStruct((1, k), f32),
            jax.ShapeDtypeStruct((1, 1), f32),
        ),
        in_specs=[vmem, vmem],
        out_specs=(vmem,) * 4,
    )(recon, c)
    return recon, grad.transpose(2, 0, 1), grad_hidden.reshape(k), grad_visible.reshape(())


def solution(mesh):
    in_specs = (P("img", "row", "col"), P(), P(), P(), P("img", "row", "col"))
    out_specs = (P("img", "row", "col"), P(), P(), P())
    return jax.shard_map(body, mesh=mesh, in_specs=in_specs, out_specs=out_specs, check_vma=False)
```

```python
import functools

import jax
import jax.numpy as jnp
from jax import lax
from jax.experimental import pallas as pl
from jax.experimental.pallas import tpu as pltpu
from jax.sharding import PartitionSpec as P

LANES = 128
MESH = pl.DeviceIdType.MESH
DIRS = [(dr, dc) for dr in (-1, 0, 1) for dc in (-1, 0, 1) if (dr, dc) != (0, 0)]
f32 = jnp.float32
bf16 = jnp.bfloat16


def slot_of(dr, dc):
    return (dr + 1) * 3 + dc + 1


def pooled(e):
    rows = e.shape[0]
    s = e + pltpu.roll(e, LANES // 2, axis=1)
    s3 = s.reshape(rows // 8, 8, LANES)
    even = lax.broadcasted_iota(jnp.int32, s3.shape, 1) % 2 == 0
    t3 = jnp.where(even, pltpu.roll(s3, 7, axis=1), pltpu.roll(s3, 1, axis=1))
    return 1.0 + s + t3.reshape(rows, LANES)


def kernel(
    geo, img_hbm, fil_hbm, hb_hbm, vb_hbm, noise_hbm, recon_ref, c_out_ref,
    img_ref, fil_ref, hb_ref, vb_ref, noise_ref, in_sem, pf, pack, recv_img, ext, a_ref, fp, tz, w_ref, h_ref, s_ref, u_ref, e_ref, recv_e,
    g_ref, acc_ref, c_ref, recv1, recv2, is_sem, ir_sem, es_sem, er_sem, s1_sem, r1_sem, s2_sem, r2_sem,
):
    ni, th, tw, k, filt, n_img, n_row, n_col = geo
    m = filt // 2
    eh, ew = th + 2 * m, tw + 2 * m
    stride = LANES // ni
    rows = ni * th
    blocks = tw * k // LANES
    kp = a_ref.shape[1]
    img_at, row_at, col_at = lax.axis_index("img"), lax.axis_index("row"), lax.axis_index("col")
    n1, n2 = n_img * n_row, n_col
    me1, me2 = img_at * n_row + row_at, col_at

    def exists(dr, dc):
        ok = True
        if dr:
            ok = (row_at > 0) if dr < 0 else (row_at < n_row - 1)
        if dc:
            ok2 = (col_at > 0) if dc < 0 else (col_at < n_col - 1)
            ok = jnp.logical_and(ok, ok2) if dr else ok2
        return ok

    def neighbour(dr, dc):
        return {"row": row_at + dr, "col": col_at + dc}

    def group1(d):
        other = lax.rem(me1 + d, n1)
        return other, {"img": other // n_row, "row": lax.rem(other, n_row)}

    def group2(d):
        other = lax.rem(me2 + d, n2)
        return other, {"col": other}

    loads = [
        pltpu.make_async_copy(src, dst, in_sem.at[i])
        for i, (src, dst) in enumerate(
            [(img_hbm, img_ref), (fil_hbm, fil_ref), (noise_hbm, noise_ref), (hb_hbm, hb_ref), (vb_hbm, vb_ref)]
        )
    ]
    for load in loads:
        load.start()

    recv_img[...] = jnp.zeros_like(recv_img)
    recv_e[...] = jnp.zeros_like(recv_e)
    barrier = pltpu.get_barrier_semaphore()
    count = jnp.int32(n1 - 1 + n2 - 1)
    for d in DIRS:
        @pl.when(exists(*d))
        def _(d=d):
            pl.semaphore_signal(barrier, inc=1, device_id=neighbour(*d), device_id_type=MESH)
        count = count + exists(*d).astype(jnp.int32)
    for d in range(1, n1):
        pl.semaphore_signal(barrier, inc=1, device_id=group1(d)[1], device_id_type=MESH)
    for d in range(1, n2):
        pl.semaphore_signal(barrier, inc=1, device_id=group2(d)[1], device_id_type=MESH)

    pf[...] = jnp.zeros_like(pf)
    fp[...] = jnp.zeros_like(fp)
    a_ref[...] = jnp.zeros_like(a_ref)
    loads[0].wait()
    for n in range(ni):
        pf[:, n * stride + m : n * stride + m + tw] = img_ref[n].astype(f32)
    pack[...] = pf[...].astype(bf16)

    top = fp.shape[0] - kp
    per = LANES // k
    loads[1].wait()
    for r in range(filt):
        fv = fil_ref[r].astype(f32)
        for jp in range(per):
            fp[top + jp + r * ew : top + jp + r * ew + filt, jp * k : (jp + 1) * k] = fv
    pl.semaphore_wait(barrier, count)

    def img_copy(dr, dc, start):
        at = slot_of(-dr, -dc) if start else slot_of(dr, dc)
        return pltpu.make_async_remote_copy(
            src_ref=pack, dst_ref=recv_img.at[at], send_sem=is_sem.at[at], recv_sem=ir_sem.at[at],
            device_id=neighbour(dr, dc), device_id_type=MESH,
        )

    for d in DIRS:
        @pl.when(exists(*d))
        def _(d=d):
            img_copy(*d, True).start()

    loads[2].wait()
    loads[3].wait()
    loads[4].wait()
    for b in range(blocks):
        tz[:, b * LANES : (b + 1) * LANES] = fp[top - per * b : top - per * b + kp, :].astype(bf16)
        w_ref[:, b * LANES : (b + 1) * LANES] = 1.0 / jnp.log(noise_ref[:, b * LANES : (b + 1) * LANES].astype(f32))

    lane = lax.broadcasted_iota(jnp.int32, (th, LANES), 1) % stride

    def place(a_row):
        for n in range(ni):
            for r in range(filt):
                a_ref[a_row + n * th : a_row + (n + 1) * th, r * ew : (r + 1) * ew] = ext[
                    r : r + th, n * stride : n * stride + ew
                ]

    for d in DIRS:
        @pl.when(exists(*d))
        def _(d=d):
            img_copy(*d, True).wait_send()
            img_copy(*d, False).wait_recv()

    for dr in (-1, 0, 1):
        centre = pf[...] if dr == 0 else recv_img[slot_of(dr, 0)].astype(f32)
        left = pltpu.roll(recv_img[slot_of(dr, -1)].astype(f32), LANES - tw, axis=1)
        right = pltpu.roll(recv_img[slot_of(dr, 1)].astype(f32), tw, axis=1)
        band = jnp.where(lane < m, left, jnp.where(lane < m + tw, centre, jnp.where(lane < ew, right, 0.0)))
        if dr == 0:
            ext[m : m + th, :] = band
        elif dr < 0:
            ext[0:m, :] = band[th - m :, :]
        else:
            ext[m + th :, :] = band[:m, :]
    place(0)

    bias = jnp.concatenate([hb_ref[...]] * per, axis=1)
    a_pos = a_ref[0:rows, :].astype(bf16)
    hidden = jnp.zeros((8, LANES), f32)

    def fold(x):
        return jnp.sum(x.reshape(rows // 8, 8, LANES), axis=0)

    step = 2 * LANES if blocks % 2 == 0 else LANES
    for b0 in range(0, blocks * LANES, step):
        xw = jnp.dot(a_pos, tz[:, b0 : b0 + step], preferred_element_type=f32)
        for o in range(0, step, LANES):
            at = b0 + o
            e = jnp.exp(xw[:, o : o + LANES] + bias)
            prob = e / pooled(e)
            hidden = hidden + fold(prob)
            h_ref[0:rows, at : at + LANES] = prob.astype(bf16)
            t = e * w_ref[:, at : at + LANES]
            t = t * t
            s_ref[:, at : at + LANES] = (t / pooled(t)).astype(bf16)

    u_ref[...] = lax.dot_general(s_ref[...], tz[...], (((1,), (1,)), ((), ())), preferred_element_type=f32)
    e_ref[...] = jnp.zeros_like(e_ref)
    gap = jnp.zeros((th, stride - ew), f32)
    for r in range(filt):
        pieces = []
        for n in range(ni):
            pieces += [u_ref[n * th : (n + 1) * th, r * ew : (r + 1) * ew], gap]
        e_ref[r : r + th, :] += jnp.concatenate(pieces, axis=1)

    def e_copy(dr, dc, start):
        at = slot_of(-dr, -dc) if start else slot_of(dr, dc)
        way = dr if start else -dr
        if way == 0:
            src, dst = e_ref, recv_e.at[at]
        elif way > 0:
            src, dst = e_ref.at[th:eh], recv_e.at[at, 0 : 2 * m]
        else:
            src, dst = e_ref.at[0 : 2 * m], recv_e.at[at, th:eh]
        return pltpu.make_async_remote_copy(
            src_ref=src, dst_ref=dst, send_sem=es_sem.at[at], recv_sem=er_sem.at[at],
            device_id=neighbour(dr, dc), device_id_type=MESH,
        )

    for d in DIRS:
        @pl.when(exists(*d))
        def _(d=d):
            e_copy(*d, True).start()
    for d in DIRS:
        @pl.when(exists(*d))
        def _(d=d):
            e_copy(*d, True).wait_send()
            e_copy(*d, False).wait_recv()

    elane = lax.broadcasted_iota(jnp.int32, (eh, LANES), 1) % stride
    erow = lax.broadcasted_iota(jnp.int32, (eh, LANES), 0)
    total = e_ref[...] + recv_e[slot_of(-1, 0)] + recv_e[slot_of(1, 0)]
    left = recv_e[slot_of(-1, -1)] + recv_e[slot_of(0, -1)] + recv_e[slot_of(1, -1)]
    right = recv_e[slot_of(-1, 1)] + recv_e[slot_of(0, 1)] + recv_e[slot_of(1, 1)]
    total = total + jnp.where(elane < 2 * m, pltpu.roll(left, LANES - tw, axis=1), 0.0)
    total = total + jnp.where(
        jnp.logical_and(elane >= tw, elane < ew), pltpu.roll(right, tw, axis=1), 0.0
    )
    recon = (total + vb_ref[...]).astype(bf16).astype(f32)
    lo_r = jnp.where(row_at == 0, m, 0)
    hi_r = jnp.where(row_at == n_row - 1, m + th, eh)
    lo_c = jnp.where(col_at == 0, m, 0)
    hi_c = jnp.where(col_at == n_col - 1, m + tw, ew)
    inside = (erow >= lo_r) & (erow < hi_r) & (elane >= lo_c) & (elane < hi_c)
    ext[...] = jnp.where(inside, recon, 0.0)
    own = ext[m : m + th, :]
    for n in range(ni):
        recon_ref[n] = own[:, n * stride + m : n * stride + m + tw].astype(bf16)
    mine = jnp.logical_and(lane >= m, lane < m + tw)
    visible = jnp.sum(jnp.where(mine, pf[...] - own, 0.0))
    place(rows)

    a_neg = a_ref[rows : 2 * rows, :].astype(bf16)
    for b0 in range(0, blocks * LANES, step):
        xw = jnp.dot(a_neg, tz[:, b0 : b0 + step], preferred_element_type=f32)
        for o in range(0, step, LANES):
            at = b0 + o
            e = jnp.exp(xw[:, o : o + LANES] + bias)
            prob = e / pooled(e)
            hidden = hidden - fold(prob)
            h_ref[rows : 2 * rows, at : at + LANES] = (-prob).astype(bf16)

    a_all = a_ref[...].astype(bf16)
    q_len = acc_ref.shape[0]
    acc = None
    for b0 in range(0, blocks * LANES, step):
        g_ref[...] = lax.dot_general(
            a_all, h_ref[:, b0 : b0 + step], (((0,), (0,)), ((), ())), preferred_element_type=f32
        )
        for o in range(0, step, LANES):
            sh = per * ((b0 + o) // LANES)
            part = g_ref[sh : sh + q_len, o : o + LANES]
            acc = part if acc is None else acc + part
    acc_ref[...] = acc
    half = -(-filt // per)
    c_ref[...] = jnp.zeros_like(c_ref)
    for r in range(filt):
        piece = acc_ref[r * ew : r * ew + filt, 0:k]
        for jp in range(1, per):
            piece = piece + acc_ref[r * ew + jp : r * ew + jp + filt, jp * k : (jp + 1) * k]
        at, rr = r // half, r % half
        c_ref[rr * filt : (rr + 1) * filt, at * k : (at + 1) * k] = piece
    hid = jnp.sum(hidden, axis=0, keepdims=True)
    hid = hid + pltpu.roll(hid, LANES // 2, axis=1)
    lane1 = lax.broadcasted_iota(jnp.int32, (1, LANES), 1)
    c_ref[half * filt : half * filt + 1, :] = jnp.where(lane1 < k, hid, jnp.where(lane1 == k, visible, 0.0))

    recv1[me1] = c_ref[...]

    def all_sum(buf, me, size, group, ssem, rsem):
        def copy(d, start):
            other, dev = group(d if start else size - d)
            at = me if start else other
            return pltpu.make_async_remote_copy(
                src_ref=buf.at[me], dst_ref=buf.at[at], send_sem=ssem.at[d], recv_sem=rsem.at[at],
                device_id=dev, device_id_type=MESH,
            )

        for d in range(1, size):
            copy(d, True).start()
        for d in range(1, size):
            copy(d, True).wait_send()
            copy(d, False).wait_recv()
        out = buf[0]
        for i in range(1, size):
            out = out + buf[i]
        return out

    recv2[me2] = all_sum(recv1, me1, n1, group1, s1_sem, r1_sem)
    scale = 1.0 / float(ni * th * tw * n_img * n_row * n_col)
    c_out_ref[...] = all_sum(recv2, me2, n2, group2, s2_sem, r2_sem) * scale


def unpack(geo, recon_in, c_ref, recon_ref, grad_ref, gh_ref, gv_ref):
    filt, k = geo
    half = -(-filt // (LANES // k))
    recon_ref[...] = recon_in[...]
    for r in range(filt):
        at, rr = r // half, r % half
        grad_ref[r] = c_ref[rr * filt : (rr + 1) * filt, at * k : (at + 1) * k]
    gh_ref[...] = c_ref[half * filt : half * filt + 1, 0:k]
    gv_ref[...] = c_ref[half * filt : half * filt + 1, k : k + 1]


def body(images, filters, hidden_bias, visible_unit_bias, unit_noise):
    ni, th, tw = images.shape
    k, filt, _ = filters.shape
    m = filt // 2
    eh, ew = th + 2 * m, tw + 2 * m
    n_img, n_row, n_col = lax.axis_size("img"), lax.axis_size("row"), lax.axis_size("col")
    rows, wide = ni * th, tw * k
    q = filt * ew
    kp = -(-q // LANES) * LANES
    per = LANES // k
    half = -(-filt // per)
    c_rows = -(-(half * filt + 1) // 8) * 8
    q_len = -(-((filt - 1) * ew + filt + per) // 8) * 8
    top = -(-tw // 16) * 16
    step = 2 * LANES if (wide // LANES) % 2 == 0 else LANES
    n1, n2 = n_img * n_row, n_col
    vmem = pl.BlockSpec(memory_space=pltpu.VMEM)
    hbm = pl.BlockSpec(memory_space=pl.ANY)
    recon, c = pl.pallas_call(
        functools.partial(kernel, (ni, th, tw, k, filt, n_img, n_row, n_col)),
        out_shape=(
            pltpu.VMEM((ni, th, tw), bf16),
            pltpu.VMEM((c_rows, LANES), f32),
        ),
        in_specs=[hbm] * 5,
        out_specs=(vmem, vmem),
        scratch_shapes=[
            pltpu.VMEM((ni, th, tw), bf16),
            pltpu.VMEM((filt, filt, k), bf16),
            pltpu.VMEM((1, k), f32),
            pltpu.VMEM((1, 1), f32),
            pltpu.VMEM((rows, wide), bf16),
            pltpu.SemaphoreType.DMA((5,)),
            pltpu.VMEM((th, LANES), f32),
            pltpu.VMEM((th, LANES), bf16),
            pltpu.VMEM((9, th, LANES), bf16),
            pltpu.VMEM((eh, LANES), f32),
            pltpu.VMEM((2 * rows, kp), f32),
            pltpu.VMEM((top + kp, LANES), f32),
            pltpu.VMEM((kp, wide), bf16),
            pltpu.VMEM((rows, wide), f32),
            pltpu.VMEM((2 * rows, wide), bf16),
            pltpu.VMEM((rows, wide), bf16),
            pltpu.VMEM((rows, kp), f32),
            pltpu.VMEM((eh, LANES), f32),
            pltpu.VMEM((9, eh, LANES), f32),
            pltpu.VMEM((kp, step), f32),
            pltpu.VMEM((q_len, LANES), f32),
            pltpu.VMEM((c_rows, LANES), f32),
            pltpu.VMEM((n1, c_rows, LANES), f32),
            pltpu.VMEM((n2, c_rows, LANES), f32),
            pltpu.SemaphoreType.DMA((9,)),
            pltpu.SemaphoreType.DMA((9,)),
            pltpu.SemaphoreType.DMA((9,)),
            pltpu.SemaphoreType.DMA((9,)),
            pltpu.SemaphoreType.DMA((n1,)),
            pltpu.SemaphoreType.DMA((n1,)),
            pltpu.SemaphoreType.DMA((n2,)),
            pltpu.SemaphoreType.DMA((n2,)),
        ],
        compiler_params=pltpu.CompilerParams(collective_id=0, has_side_effects=True),
    )(
        images,
        filters.transpose(1, 2, 0),
        hidden_bias.reshape(1, k),
        visible_unit_bias.reshape(1, 1),
        unit_noise.reshape(rows, wide),
    )
    recon, grad, grad_hidden, grad_visible = pl.pallas_call(
        functools.partial(unpack, (filt, k)),
        out_shape=(
            jax.ShapeDtypeStruct((ni, th, tw), bf16),
            jax.ShapeDtypeStruct((filt, filt, k), f32),
            jax.ShapeDtypeStruct((1, k), f32),
            jax.ShapeDtypeStruct((1, 1), f32),
        ),
        in_specs=[vmem, vmem],
        out_specs=(vmem,) * 4,
    )(*[pltpu.with_memory_space_constraint(x, pltpu.VMEM) for x in (recon, c)])
    return recon, grad.transpose(2, 0, 1), grad_hidden.reshape(k), grad_visible.reshape(())


def solution(mesh):
    in_specs = (P("img", "row", "col"), P(), P(), P(), P("img", "row", "col"))
    out_specs = (P("img", "row", "col"), P(), P(), P())
    return jax.shard_map(body, mesh=mesh, in_specs=in_specs, out_specs=out_specs, check_vma=False)
```

```python
import functools

import jax
import jax.numpy as jnp
from jax import lax
from jax.experimental import pallas as pl
from jax.experimental.pallas import tpu as pltpu
from jax.sharding import PartitionSpec as P

LANES = 128
MESH = pl.DeviceIdType.MESH
DIRS = [(dr, dc) for dr in (-1, 0, 1) for dc in (-1, 0, 1) if (dr, dc) != (0, 0)]
f32 = jnp.float32
bf16 = jnp.bfloat16


def slot_of(dr, dc):
    return (dr + 1) * 3 + dc + 1


def pooled(e):
    rows = e.shape[0]
    s = e + pltpu.roll(e, LANES // 2, axis=1)
    s3 = s.reshape(rows // 8, 8, LANES)
    even = lax.broadcasted_iota(jnp.int32, s3.shape, 1) % 2 == 0
    t3 = jnp.where(even, pltpu.roll(s3, 7, axis=1), pltpu.roll(s3, 1, axis=1))
    return 1.0 + s + t3.reshape(rows, LANES)


def kernel(
    geo, img_hbm, fil_hbm, hb_hbm, vb_hbm, noise_hbm, recon_ref, c_out_ref,
    img_ref, fil_ref, hb_ref, vb_ref, noise_ref, in_sem, pf, pack, recv_img, ext, a_ref, fp, tz, w_ref, h_ref, s_ref, u_ref, e_ref, recv_e,
    g_ref, acc_ref, call_ref, c_ref, recv1, recv2, recv3, is_sem, ir_sem, es_sem, er_sem, s1_sem, r1_sem, s2_sem, r2_sem, s3_sem, r3_sem,
):
    ni, th, tw, k, filt, n_img, n_row, n_col = geo
    m = filt // 2
    eh, ew = th + 2 * m, tw + 2 * m
    stride = LANES // ni
    rows = ni * th
    blocks = tw * k // LANES
    kp = a_ref.shape[1]
    img_at, row_at, col_at = lax.axis_index("img"), lax.axis_index("row"), lax.axis_index("col")
    n1, n2 = n_img * n_row, n_col
    me1, me2 = img_at * n_row + row_at, col_at

    def exists(dr, dc):
        ok = True
        if dr:
            ok = (row_at > 0) if dr < 0 else (row_at < n_row - 1)
        if dc:
            ok2 = (col_at > 0) if dc < 0 else (col_at < n_col - 1)
            ok = jnp.logical_and(ok, ok2) if dr else ok2
        return ok

    def neighbour(dr, dc):
        return {"row": row_at + dr, "col": col_at + dc}

    def group1(d):
        other = lax.rem(me1 + d, n1)
        return other, {"img": other // n_row, "row": lax.rem(other, n_row)}

    def group2(d):
        other = lax.rem(me2 + d, n2)
        return other, {"col": other}

    loads = [
        pltpu.make_async_copy(src, dst, in_sem.at[i])
        for i, (src, dst) in enumerate(
            [(img_hbm, img_ref), (fil_hbm, fil_ref), (noise_hbm, noise_ref), (hb_hbm, hb_ref), (vb_hbm, vb_ref)]
        )
    ]
    for load in loads:
        load.start()

    recv_img[...] = jnp.zeros_like(recv_img)
    recv_e[...] = jnp.zeros_like(recv_e)
    barrier = pltpu.get_barrier_semaphore()
    count = jnp.int32(n1 - 1 + n2 - 1)
    for d in DIRS:
        @pl.when(exists(*d))
        def _(d=d):
            pl.semaphore_signal(barrier, inc=1, device_id=neighbour(*d), device_id_type=MESH)
        count = count + exists(*d).astype(jnp.int32)
    for d in range(1, n1):
        pl.semaphore_signal(barrier, inc=1, device_id=group1(d)[1], device_id_type=MESH)
    for d in range(1, n2):
        pl.semaphore_signal(barrier, inc=1, device_id=group2(d)[1], device_id_type=MESH)

    pf[...] = jnp.zeros_like(pf)
    fp[...] = jnp.zeros_like(fp)
    a_ref[...] = jnp.zeros_like(a_ref)
    loads[0].wait()
    for n in range(ni):
        pf[:, n * stride + m : n * stride + m + tw] = img_ref[n].astype(f32)
    pack[...] = pf[...].astype(bf16)

    top = fp.shape[0] - kp
    per = LANES // k
    loads[1].wait()
    for r in range(filt):
        fv = fil_ref[r].astype(f32)
        for jp in range(per):
            fp[top + jp + r * ew : top + jp + r * ew + filt, jp * k : (jp + 1) * k] = fv
    pl.semaphore_wait(barrier, count)

    def img_copy(dr, dc, start):
        at = slot_of(-dr, -dc) if start else slot_of(dr, dc)
        return pltpu.make_async_remote_copy(
            src_ref=pack, dst_ref=recv_img.at[at], send_sem=is_sem.at[at], recv_sem=ir_sem.at[at],
            device_id=neighbour(dr, dc), device_id_type=MESH,
        )

    for d in DIRS:
        @pl.when(exists(*d))
        def _(d=d):
            img_copy(*d, True).start()

    loads[2].wait()
    loads[3].wait()
    loads[4].wait()
    for b in range(blocks):
        tz[:, b * LANES : (b + 1) * LANES] = fp[top - per * b : top - per * b + kp, :].astype(bf16)
        w_ref[:, b * LANES : (b + 1) * LANES] = 1.0 / jnp.log(noise_ref[:, b * LANES : (b + 1) * LANES].astype(f32))

    lane = lax.broadcasted_iota(jnp.int32, (th, LANES), 1) % stride

    def place(a_row):
        for n in range(ni):
            for r in range(filt):
                a_ref[a_row + n * th : a_row + (n + 1) * th, r * ew : (r + 1) * ew] = ext[
                    r : r + th, n * stride : n * stride + ew
                ]

    for d in DIRS:
        @pl.when(exists(*d))
        def _(d=d):
            img_copy(*d, True).wait_send()
            img_copy(*d, False).wait_recv()

    for dr in (-1, 0, 1):
        centre = pf[...] if dr == 0 else recv_img[slot_of(dr, 0)].astype(f32)
        left = pltpu.roll(recv_img[slot_of(dr, -1)].astype(f32), LANES - tw, axis=1)
        right = pltpu.roll(recv_img[slot_of(dr, 1)].astype(f32), tw, axis=1)
        band = jnp.where(lane < m, left, jnp.where(lane < m + tw, centre, jnp.where(lane < ew, right, 0.0)))
        if dr == 0:
            ext[m : m + th, :] = band
        elif dr < 0:
            ext[0:m, :] = band[th - m :, :]
        else:
            ext[m + th :, :] = band[:m, :]
    place(0)

    bias = jnp.concatenate([hb_ref[...]] * per, axis=1)
    a_pos = a_ref[0:rows, :].astype(bf16)
    hidden = jnp.zeros((8, LANES), f32)

    def fold(x):
        return jnp.sum(x.reshape(rows // 8, 8, LANES), axis=0)

    step = 2 * LANES if blocks % 2 == 0 else LANES
    for b0 in range(0, blocks * LANES, step):
        xw = jnp.dot(a_pos, tz[:, b0 : b0 + step], preferred_element_type=f32)
        for o in range(0, step, LANES):
            at = b0 + o
            e = jnp.exp(xw[:, o : o + LANES] + bias)
            prob = e / pooled(e)
            hidden = hidden + fold(prob)
            h_ref[0:rows, at : at + LANES] = prob.astype(bf16)
            t = e * w_ref[:, at : at + LANES]
            t = t * t
            s_ref[:, at : at + LANES] = (t / pooled(t)).astype(bf16)

    u_ref[...] = lax.dot_general(s_ref[...], tz[...], (((1,), (1,)), ((), ())), preferred_element_type=f32)
    e_ref[...] = jnp.zeros_like(e_ref)
    gap = jnp.zeros((th, stride - ew), f32)
    for r in range(filt):
        pieces = []
        for n in range(ni):
            pieces += [u_ref[n * th : (n + 1) * th, r * ew : (r + 1) * ew], gap]
        e_ref[r : r + th, :] += jnp.concatenate(pieces, axis=1)

    def e_copy(dr, dc, start):
        at = slot_of(-dr, -dc) if start else slot_of(dr, dc)
        way = dr if start else -dr
        if way == 0:
            src, dst = e_ref, recv_e.at[at]
        elif way > 0:
            src, dst = e_ref.at[th:eh], recv_e.at[at, 0 : 2 * m]
        else:
            src, dst = e_ref.at[0 : 2 * m], recv_e.at[at, th:eh]
        return pltpu.make_async_remote_copy(
            src_ref=src, dst_ref=dst, send_sem=es_sem.at[at], recv_sem=er_sem.at[at],
            device_id=neighbour(dr, dc), device_id_type=MESH,
        )

    for d in DIRS:
        @pl.when(exists(*d))
        def _(d=d):
            e_copy(*d, True).start()
    for d in DIRS:
        @pl.when(exists(*d))
        def _(d=d):
            e_copy(*d, True).wait_send()
            e_copy(*d, False).wait_recv()

    elane = lax.broadcasted_iota(jnp.int32, (eh, LANES), 1) % stride
    erow = lax.broadcasted_iota(jnp.int32, (eh, LANES), 0)
    total = e_ref[...] + recv_e[slot_of(-1, 0)] + recv_e[slot_of(1, 0)]
    left = recv_e[slot_of(-1, -1)] + recv_e[slot_of(0, -1)] + recv_e[slot_of(1, -1)]
    right = recv_e[slot_of(-1, 1)] + recv_e[slot_of(0, 1)] + recv_e[slot_of(1, 1)]
    total = total + jnp.where(elane < 2 * m, pltpu.roll(left, LANES - tw, axis=1), 0.0)
    total = total + jnp.where(
        jnp.logical_and(elane >= tw, elane < ew), pltpu.roll(right, tw, axis=1), 0.0
    )
    recon = (total + vb_ref[...]).astype(bf16).astype(f32)
    lo_r = jnp.where(row_at == 0, m, 0)
    hi_r = jnp.where(row_at == n_row - 1, m + th, eh)
    lo_c = jnp.where(col_at == 0, m, 0)
    hi_c = jnp.where(col_at == n_col - 1, m + tw, ew)
    inside = (erow >= lo_r) & (erow < hi_r) & (elane >= lo_c) & (elane < hi_c)
    ext[...] = jnp.where(inside, recon, 0.0)
    own = ext[m : m + th, :]
    for n in range(ni):
        recon_ref[n] = own[:, n * stride + m : n * stride + m + tw].astype(bf16)
    mine = jnp.logical_and(lane >= m, lane < m + tw)
    visible = jnp.sum(jnp.where(mine, pf[...] - own, 0.0))
    place(rows)

    a_neg = a_ref[rows : 2 * rows, :].astype(bf16)
    for b0 in range(0, blocks * LANES, step):
        xw = jnp.dot(a_neg, tz[:, b0 : b0 + step], preferred_element_type=f32)
        for o in range(0, step, LANES):
            at = b0 + o
            e = jnp.exp(xw[:, o : o + LANES] + bias)
            prob = e / pooled(e)
            hidden = hidden - fold(prob)
            h_ref[rows : 2 * rows, at : at + LANES] = (-prob).astype(bf16)

    a_all = a_ref[...].astype(bf16)
    q_len = acc_ref.shape[0]
    acc = None
    for b0 in range(0, blocks * LANES, step):
        g_ref[...] = lax.dot_general(
            a_all, h_ref[:, b0 : b0 + step], (((0,), (0,)), ((), ())), preferred_element_type=f32
        )
        for o in range(0, step, LANES):
            sh = per * ((b0 + o) // LANES)
            part = g_ref[sh : sh + q_len, o : o + LANES]
            acc = part if acc is None else acc + part
    acc_ref[...] = acc
    half = -(-filt // per)
    call_ref[...] = jnp.zeros_like(call_ref)
    for r in range(filt):
        piece = acc_ref[r * ew : r * ew + filt, 0:k]
        for jp in range(1, per):
            piece = piece + acc_ref[r * ew + jp : r * ew + jp + filt, jp * k : (jp + 1) * k]
        at, rr = r // half, r % half
        call_ref[rr * filt : (rr + 1) * filt, at * k : (at + 1) * k] = piece
    hid = jnp.sum(hidden, axis=0, keepdims=True)
    hid = hid + pltpu.roll(hid, LANES // 2, axis=1)
    lane1 = lax.broadcasted_iota(jnp.int32, (1, LANES), 1)
    call_ref[half * filt : half * filt + 1, :] = jnp.where(lane1 < k, hid, jnp.where(lane1 == k, visible, 0.0))
    for i in range(n_img):
        c_ref[i] = call_ref[i * c_ref.shape[1] : (i + 1) * c_ref.shape[1], :]

    deep = recv1.shape[1]

    def give1(d):
        other, dev = group1(d)
        return other, dev, lax.div(other, n_row)

    def send(src, dst, ssem, rsem, dev):
        return pltpu.make_async_remote_copy(
            src_ref=src, dst_ref=dst, send_sem=ssem, recv_sem=rsem, device_id=dev, device_id_type=MESH
        )

    for d in range(1, n1):
        other, dev, part = give1(d)
        send(c_ref.at[part], recv1.at[me1], s1_sem.at[d], r1_sem.at[me1], dev).start()
    recv1[me1] = c_ref[img_at]
    for d in range(1, n1):
        other, dev, part = give1(d)
        send(c_ref.at[part], recv1.at[other], s1_sem.at[d], r1_sem.at[other], dev).wait_recv()
    out = recv1[0]
    for i in range(1, n1):
        out = out + recv1[i]
    recv2[me2] = out
    for d in range(1, n2):
        other, dev = group2(d)
        send(recv2.at[me2], recv2.at[me2], s2_sem.at[d], r2_sem.at[me2], dev).start()
    for d in range(1, n2):
        other, dev = group2(d)
        send(recv2.at[me2], recv2.at[other], s2_sem.at[d], r2_sem.at[other], dev).wait_recv()
    out = recv2[0]
    for i in range(1, n2):
        out = out + recv2[i]
    scale = 1.0 / float(ni * th * tw * n_img * n_row * n_col)
    recv3[img_at] = out * scale

    def group3(d):
        other = lax.rem(img_at + d, n_img)
        return other, {"img": other}

    for d in range(1, n_img):
        other, dev = group3(d)
        send(recv3.at[img_at], recv3.at[img_at], s3_sem.at[d], r3_sem.at[img_at], dev).start()
    for d in range(1, n_img):
        other, dev = group3(d)
        send(recv3.at[img_at], recv3.at[other], s3_sem.at[d], r3_sem.at[other], dev).wait_recv()
    for i in range(n_img):
        c_out_ref[i * deep : (i + 1) * deep, :] = recv3[i]
    for d in range(1, n1):
        other, dev, part = give1(d)
        send(c_ref.at[part], recv1.at[me1], s1_sem.at[d], r1_sem.at[me1], dev).wait_send()
    for d in range(1, n2):
        other, dev = group2(d)
        send(recv2.at[me2], recv2.at[me2], s2_sem.at[d], r2_sem.at[me2], dev).wait_send()
    for d in range(1, n_img):
        other, dev = group3(d)
        send(recv3.at[img_at], recv3.at[img_at], s3_sem.at[d], r3_sem.at[img_at], dev).wait_send()


def unpack(geo, recon_in, c_ref, recon_ref, grad_ref, gh_ref, gv_ref):
    filt, k = geo
    half = -(-filt // (LANES // k))
    recon_ref[...] = recon_in[...]
    for r in range(filt):
        at, rr = r // half, r % half
        grad_ref[r] = c_ref[rr * filt : (rr + 1) * filt, at * k : (at + 1) * k]
    gh_ref[...] = c_ref[half * filt : half * filt + 1, 0:k]
    gv_ref[...] = c_ref[half * filt : half * filt + 1, k : k + 1]


def body(images, filters, hidden_bias, visible_unit_bias, unit_noise):
    ni, th, tw = images.shape
    k, filt, _ = filters.shape
    m = filt // 2
    eh, ew = th + 2 * m, tw + 2 * m
    n_img, n_row, n_col = lax.axis_size("img"), lax.axis_size("row"), lax.axis_size("col")
    rows, wide = ni * th, tw * k
    q = filt * ew
    kp = -(-q // LANES) * LANES
    per = LANES // k
    half = -(-filt // per)
    c_rows = -(-(half * filt + 1) // (8 * n_img)) * 8 * n_img
    q_len = -(-((filt - 1) * ew + filt + per) // 8) * 8
    top = -(-tw // 16) * 16
    step = 2 * LANES if (wide // LANES) % 2 == 0 else LANES
    n1, n2 = n_img * n_row, n_col
    vmem = pl.BlockSpec(memory_space=pltpu.VMEM)
    hbm = pl.BlockSpec(memory_space=pl.ANY)
    recon, c = pl.pallas_call(
        functools.partial(kernel, (ni, th, tw, k, filt, n_img, n_row, n_col)),
        out_shape=(
            pltpu.VMEM((ni, th, tw), bf16),
            pltpu.VMEM((c_rows, LANES), f32),
        ),
        in_specs=[hbm] * 5,
        out_specs=(vmem, vmem),
        scratch_shapes=[
            pltpu.VMEM((ni, th, tw), bf16),
            pltpu.VMEM((filt, filt, k), bf16),
            pltpu.VMEM((1, k), f32),
            pltpu.VMEM((1, 1), f32),
            pltpu.VMEM((rows, wide), bf16),
            pltpu.SemaphoreType.DMA((5,)),
            pltpu.VMEM((th, LANES), f32),
            pltpu.VMEM((th, LANES), bf16),
            pltpu.VMEM((9, th, LANES), bf16),
            pltpu.VMEM((eh, LANES), f32),
            pltpu.VMEM((2 * rows, kp), f32),
            pltpu.VMEM((top + kp, LANES), f32),
            pltpu.VMEM((kp, wide), bf16),
            pltpu.VMEM((rows, wide), f32),
            pltpu.VMEM((2 * rows, wide), bf16),
            pltpu.VMEM((rows, wide), bf16),
            pltpu.VMEM((rows, kp), f32),
            pltpu.VMEM((eh, LANES), f32),
            pltpu.VMEM((9, eh, LANES), f32),
            pltpu.VMEM((kp, step), f32),
            pltpu.VMEM((q_len, LANES), f32),
            pltpu.VMEM((c_rows, LANES), f32),
            pltpu.VMEM((n_img, c_rows // n_img, LANES), f32),
            pltpu.VMEM((n1, c_rows // n_img, LANES), f32),
            pltpu.VMEM((n2, c_rows // n_img, LANES), f32),
            pltpu.VMEM((n_img, c_rows // n_img, LANES), f32),
            pltpu.SemaphoreType.DMA((9,)),
            pltpu.SemaphoreType.DMA((9,)),
            pltpu.SemaphoreType.DMA((9,)),
            pltpu.SemaphoreType.DMA((9,)),
            pltpu.SemaphoreType.DMA((n1,)),
            pltpu.SemaphoreType.DMA((n1,)),
            pltpu.SemaphoreType.DMA((n2,)),
            pltpu.SemaphoreType.DMA((n2,)),
            pltpu.SemaphoreType.DMA((n_img,)),
            pltpu.SemaphoreType.DMA((n_img,)),
        ],
        compiler_params=pltpu.CompilerParams(collective_id=0, has_side_effects=True),
    )(
        images,
        filters.transpose(1, 2, 0),
        hidden_bias.reshape(1, k),
        visible_unit_bias.reshape(1, 1),
        unit_noise.reshape(rows, wide),
    )
    recon, grad, grad_hidden, grad_visible = pl.pallas_call(
        functools.partial(unpack, (filt, k)),
        out_shape=(
            jax.ShapeDtypeStruct((ni, th, tw), bf16),
            jax.ShapeDtypeStruct((filt, filt, k), f32),
            jax.ShapeDtypeStruct((1, k), f32),
            jax.ShapeDtypeStruct((1, 1), f32),
        ),
        in_specs=[vmem, vmem],
        out_specs=(vmem,) * 4,
    )(*[pltpu.with_memory_space_constraint(x, pltpu.VMEM) for x in (recon, c)])
    return recon, grad.transpose(2, 0, 1), grad_hidden.reshape(k), grad_visible.reshape(())


def solution(mesh):
    in_specs = (P("img", "row", "col"), P(), P(), P(), P("img", "row", "col"))
    out_specs = (P("img", "row", "col"), P(), P(), P())
    return jax.shard_map(body, mesh=mesh, in_specs=in_specs, out_specs=out_specs, check_vma=False)
```
